32 devices in a mesh: space: 4 (over y, x), exc: 8 (over z, core).
Axes of the slice: x: 2, y: 2, z: 4, core: 2. Of those that a mesh axis runs over, the one named last changes fastest.
Arguments:
- coeff: float32 [64, 256, 4096], P('space', None, 'exc'), may hold values from -6 to 6
- factors: float32 [4, 64, 256, 512], P(None, 'space', 'exc'), may hold values from -0.25 to 0.25
Outputs:
- applied: float32 [64, 256, 4096], P('space', None, 'exc')
The draws below stay inside these ranges and needn't reach their ends.
All inputs are finite; a program needn't handle non-finite values.
Results may differ from the reference program's by a relative error of at most 0.0003.
Values sent between devices are 32-bit elements; how exact they have to be, the bound alone decides.
A program may use at most 128 MiB of HBM per device.

```python
import jax
import jax.numpy as jnp
from jax import lax

BLOCKS = 64
BITS = 6
RANK = 256
LEVELS = 4
EXC = 4096


def levels(key, extent, pieces, low, top_value):
    factor_of, own = 1.0, jax.random.fold_in(key, 6)
    for axis_at, blocks in pieces:
        draws = jnp.exp(jax.random.uniform(jax.random.fold_in(own, axis_at), (blocks,), jnp.float32, low / len(pieces), top_value / len(pieces)))
        factor_of = factor_of * jnp.repeat(draws, extent[axis_at] // blocks).reshape([-1 if axis == axis_at else 1 for axis in range(len(extent))])
    return factor_of


def scatter_about(key, dims, deviation, bound, cuts=(), kind=jnp.bfloat16):
    loudness = levels(key, dims, cuts, -0.22, 0.18) if cuts else 1.0
    drawn = jax.random.normal(key, dims, jnp.float32) * deviation * loudness
    return jnp.minimum(jnp.maximum(drawn, -bound), bound).astype(kind)


def setup_inputs(seed: int = 0) -> dict:
    streams_of = jax.random.split(jax.random.key(seed), 3)
    coeff = scatter_about(streams_of[0], (BLOCKS, RANK, EXC), 1.0, 6.0, ((0, 4), (2, 8)), jnp.float32)
    factors = scatter_about(streams_of[1], (LEVELS, BLOCKS, RANK, 2 * RANK), (2 * RANK) ** -0.5, 0.25, ((1, 4), (2, 8)), jnp.float32)
    return {"coeff": coeff, "factors": factors}


def apply_level(state, level_factors, stride):
    def one_block(index):
        upper = (index // stride) % 2
        partner = (index + stride - 2 * stride * upper).astype(jnp.int32)
        stacked = jnp.concatenate([state[index], state[partner]], axis=0)
        return jnp.dot(level_factors[index], stacked, precision=lax.Precision.HIGHEST, preferred_element_type=jnp.float32)
    return lax.map(one_block, jnp.arange(BLOCKS, dtype=jnp.int32))


def reference(coeff, factors):
    state = coeff
    for level in range(LEVELS):
        stride = 2 ** (BITS - LEVELS + level)
        state = apply_level(state, factors[level], stride)
    return state
```

```python
import functools

import jax
import jax.numpy as jnp
from jax import lax
from jax.experimental import pallas as pl
from jax.experimental.pallas import tpu as pltpu
from jax.sharding import PartitionSpec as P

BITS = 6
LEVELS = 4
CORES = 2
AHEAD = 3
TILE = 256
PHASE = (0.0, 0.1, 4.5, 14.0)
UP, DOWN, SIDE = 0, 1, 2


def split(x):
    high = x.astype(jnp.bfloat16)
    low = (x - high.astype(jnp.float32)).astype(jnp.bfloat16)
    return high, low


def dot3(a, b):
    dot = functools.partial(jnp.dot, preferred_element_type=jnp.float32)
    return dot(a[0], b[0]) + (dot(a[0], b[1]) + dot(a[1], b[0]))


def kernel(local_levels, coeff, fac, out, full, other, state, load_sem, own_sem, recv_sem, send_sem, xsend, xrecv):
    space, exc = lax.axis_index("space"), lax.axis_index("exc")
    chips = lax.axis_size("exc") // CORES
    chip, core = exc // CORES, exc % CORES
    sibling = exc + 1 - 2 * core
    nloc, groups, rank, cols = state.shape
    rows = fac.shape[3]
    tile = min(TILE, cols)
    units = sorted(
        ((level, group) for level in range(LEVELS) for group in range(groups)),
        key=lambda u: 3 * u[1] + PHASE[u[0]],
    )

    def shard(unit, source):
        level, group = units[unit]
        start = pl.multiple_of(source * rows, rows)
        return full.at[level, :, group, pl.ds(start, rows), :]

    def mine(unit):
        level, group = units[unit]
        return fac.at[level, :, group]

    def own_copy(unit):
        return pltpu.make_async_copy(mine(unit), shard(unit, exc), own_sem.at[unit])

    def remote(unit, src_ref, source, way, target):
        return pltpu.make_async_remote_copy(
            src_ref=src_ref,
            dst_ref=shard(unit, source),
            send_sem=send_sem.at[unit, way, source // CORES],
            recv_sem=recv_sem.at[unit, source],
            device_id=(space, target),
            device_id_type=pl.DeviceIdType.MESH,
        )

    def arrive(unit, source):
        remote(unit, shard(unit, source), source, SIDE, sibling).wait_recv()

    def send_own(unit):
        @pl.when(chip < chips - 1)
        def _():
            remote(unit, mine(unit), exc, UP, exc + CORES).start()

        @pl.when(chip > 0)
        def _():
            remote(unit, mine(unit), exc, DOWN, exc - CORES).start()

        remote(unit, mine(unit), exc, SIDE, sibling).start()
        own_copy(unit).start()

    def relay(unit):
        def hop(distance, carry):
            @pl.when(chip >= distance)
            def _():
                source = exc - distance * CORES
                arrive(unit, source)

                @pl.when(chip < chips - 1)
                def _():
                    remote(unit, shard(unit, source), source, UP, exc + CORES).start()

                remote(unit, shard(unit, source), source, SIDE, sibling).start()

            @pl.when(chip + distance < chips)
            def _():
                source = exc + distance * CORES
                arrive(unit, source)

                @pl.when(chip > 0)
                def _():
                    remote(unit, shard(unit, source), source, DOWN, exc - CORES).start()

                remote(unit, shard(unit, source), source, SIDE, sibling).start()

            return carry

        lax.fori_loop(1, chips, hop, 0)

    def exchange(level, group):
        at = level - local_levels
        stride = 1 << at
        partner = space + stride - 2 * stride * ((space // stride) % 2)
        return pltpu.make_async_remote_copy(
            src_ref=state.at[:, group],
            dst_ref=other.at[at, :, group],
            send_sem=xsend.at[at, group],
            recv_sem=xrecv.at[at, group],
            device_id=(partner, exc),
            device_id_type=pl.DeviceIdType.MESH,
        )

    def load(group):
        return pltpu.make_async_copy(coeff.at[:, group], state.at[:, group], load_sem.at[group])

    def store(group):
        return pltpu.make_async_copy(state.at[:, group], out.at[:, group], load_sem.at[group])

    def product(level, group, block, own, partner):
        top = split(full[level, block, group, :, :rank])
        bottom = split(full[level, block, group, :, rank:])
        return dot3(top, own) + dot3(bottom, partner)

    def consume(unit):
        level, group = units[unit]
        own_copy(unit).wait()

        def landed(index, carry):
            arrive(unit, index * CORES + 1 - core)
            return carry

        lax.fori_loop(0, chips, landed, 0)
        if level == 0:
            load(group).wait()
        tiles = cols // tile
        if level < local_levels:
            stride = 1 << level

            def pair(step, carry):
                index = step // tiles
                low = index // stride * 2 * stride + index % stride
                high = low + stride
                at = pl.ds(pl.multiple_of(step % tiles * tile, tile), tile)
                first = split(state[low, group, :, at])
                second = split(state[high, group, :, at])
                state[low, group, :, at] = product(level, group, low, first, second)
                state[high, group, :, at] = product(level, group, high, second, first)
                return carry

            lax.fori_loop(0, nloc // 2 * tiles, pair, 0)
        else:
            exchange(level, group).wait()

            def single(step, carry):
                block = step // tiles
                at = pl.ds(pl.multiple_of(step % tiles * tile, tile), tile)
                first = split(state[block, group, :, at])
                second = split(other[level - local_levels, block, group, :, at])
                state[block, group, :, at] = product(level, group, block, first, second)
                return carry

            lax.fori_loop(0, nloc * tiles, single, 0)
        if level + 1 == LEVELS:
            store(group).start()
        elif level + 1 >= local_levels:
            exchange(level + 1, group).start()

    for group in range(groups):
        load(group).start()
    for unit in range(min(AHEAD, len(units))):
        send_own(unit)
    if local_levels == 0:
        for group in range(groups):
            load(group).wait()
            exchange(0, group).start()
    held = []
    for unit in range(len(units)):
        if unit + AHEAD < len(units):
            send_own(unit + AHEAD)
        relay(unit)
        for late in held:
            consume(late)
        held = []
        if units[unit] == (LEVELS - 2, groups - 1):
            held = [unit]
        else:
            consume(unit)

    for group in range(groups):
        store(group).wait()
    for unit in range(len(units)):

        def drained(index, carry):
            source = index * CORES + core
            done = functools.partial(remote, unit, shard(unit, source), source)

            @pl.when((index <= chip) & (chip < chips - 1))
            def _():
                done(UP, sibling).wait_send()

            @pl.when((index >= chip) & (chip > 0))
            def _():
                done(DOWN, sibling).wait_send()

            done(SIDE, sibling).wait_send()
            return carry

        lax.fori_loop(0, chips, drained, 0)


def body(coeff, factors):
    blocks, rank, cols = coeff.shape
    rows, width = factors.shape[2:]
    groups = 1 << (BITS - LEVELS)
    nloc = blocks // groups
    local_levels = nloc.bit_length() - 1
    devices = lax.axis_size("exc")
    units = LEVELS * groups
    crossing = LEVELS - local_levels
    dma = pltpu.SemaphoreType.DMA
    result = pl.pallas_call(
        functools.partial(kernel, local_levels),
        out_shape=jax.ShapeDtypeStruct((nloc, groups, rank, cols), jnp.float32),
        in_specs=[pl.BlockSpec(memory_space=pl.ANY)] * 2,
        out_specs=pl.BlockSpec(memory_space=pl.ANY),
        scratch_shapes=[
            pltpu.VMEM((LEVELS, nloc, groups, rank, width), jnp.float32),
            pltpu.VMEM((crossing, nloc, groups, rank, cols), jnp.float32),
            pltpu.VMEM((nloc, groups, rank, cols), jnp.float32),
            dma((groups,)),
            dma((units,)),
            dma((units, devices)),
            dma((units, 3, devices // CORES)),
            dma((crossing, groups)),
            dma((crossing, groups)),
        ],
        compiler_params=pltpu.CompilerParams(has_side_effects=True, vmem_limit_bytes=63 << 20),
    )(
        coeff.reshape(nloc, groups, rank, cols),
        factors.reshape(LEVELS, nloc, groups, rows, width),
    )
    return result.reshape(coeff.shape)


def solution(mesh):
    return jax.shard_map(
        body,
        mesh=mesh,
        in_specs=(P("space", None, "exc"), P(None, "space", "exc", None)),
        out_specs=P("space", None, "exc"),
        check_vma=False,
    )
```

```python
import functools

import jax
import jax.numpy as jnp
from jax import lax
from jax.experimental import pallas as pl
from jax.experimental.pallas import tpu as pltpu
from jax.sharding import PartitionSpec as P

BITS = 6
LEVELS = 4
CORES = 2
AHEAD = 2
TILE = 256
PHASE = (0.0, 0.1, 4.5, 14.0)
LAG = (0, 0, 0, 0)
UP, DOWN, SIDE = 0, 1, 2


def split(x):
    high = x.astype(jnp.bfloat16)
    low = (x - high.astype(jnp.float32)).astype(jnp.bfloat16)
    return high, low


def dot3(a, b):
    dot = functools.partial(jnp.dot, preferred_element_type=jnp.float32)
    return dot(a[0], b[0]) + (dot(a[0], b[1]) + dot(a[1], b[0]))


def kernel(local_levels, coeff, fac, out, full, other, state, load_sem, store_sem, own_sem, recv_sem, send_sem, xsend, xrecv):
    space, exc = lax.axis_index("space"), lax.axis_index("exc")
    chips = lax.axis_size("exc") // CORES
    chip, core = exc // CORES, exc % CORES
    sibling = exc + 1 - 2 * core
    nloc, groups, rank, cols = state.shape
    rows = fac.shape[3]
    tile = min(TILE, cols)
    units = sorted(
        ((level, group) for level in range(LEVELS) for group in range(groups)),
        key=lambda u: 3 * u[1] + PHASE[u[0]],
    )

    def shard(unit, source):
        level, group = units[unit]
        start = pl.multiple_of(source * rows, rows)
        return full.at[level, :, group, pl.ds(start, rows), :]

    def mine(unit):
        level, group = units[unit]
        return fac.at[level, :, group]

    def own_copy(unit):
        return pltpu.make_async_copy(mine(unit), shard(unit, exc), own_sem.at[unit])

    def remote(unit, src_ref, source, way, target):
        return pltpu.make_async_remote_copy(
            src_ref=src_ref,
            dst_ref=shard(unit, source),
            send_sem=send_sem.at[unit, way, source // CORES],
            recv_sem=recv_sem.at[unit, source],
            device_id=(space, target),
            device_id_type=pl.DeviceIdType.MESH,
        )

    def arrive(unit, source):
        remote(unit, shard(unit, source), source, SIDE, sibling).wait_recv()

    def send_own(unit):
        @pl.when(chip < chips - 1)
        def _():
            remote(unit, mine(unit), exc, UP, exc + CORES).start()

        @pl.when(chip > 0)
        def _():
            remote(unit, mine(unit), exc, DOWN, exc - CORES).start()

        remote(unit, mine(unit), exc, SIDE, sibling).start()
        own_copy(unit).start()

    def relay(unit):
        def hop(distance, carry):
            @pl.when(chip >= distance)
            def _():
                source = exc - distance * CORES
                arrive(unit, source)

                @pl.when(chip < chips - 1)
                def _():
                    remote(unit, shard(unit, source), source, UP, exc + CORES).start()

                remote(unit, shard(unit, source), source, SIDE, sibling).start()

            @pl.when(chip + distance < chips)
            def _():
                source = exc + distance * CORES
                arrive(unit, source)

                @pl.when(chip > 0)
                def _():
                    remote(unit, shard(unit, source), source, DOWN, exc - CORES).start()

                remote(unit, shard(unit, source), source, SIDE, sibling).start()

            return carry

        lax.fori_loop(1, chips, hop, 0)

    def exchange(level, group, block):
        at = level - local_levels
        stride = 1 << at
        partner = space + stride - 2 * stride * ((space // stride) % 2)
        return pltpu.make_async_remote_copy(
            src_ref=state.at[block, group],
            dst_ref=other.at[at, block, group],
            send_sem=xsend.at[at, group, block],
            recv_sem=xrecv.at[at, group, block],
            device_id=(partner, exc),
            device_id_type=pl.DeviceIdType.MESH,
        )

    def load(group):
        return pltpu.make_async_copy(coeff.at[:, group], state.at[:, group], load_sem.at[group])

    def store(group, block):
        return pltpu.make_async_copy(
            state.at[block, group], out.at[block, group], store_sem.at[group, block]
        )

    def pass_on(level, group, block):
        if level + 1 == LEVELS:
            store(group, block).start()
        elif level + 1 >= local_levels:
            exchange(level + 1, group, block).start()

    def product(level, group, block, own, partner):
        top = split(full[level, block, group, :, :rank])
        bottom = split(full[level, block, group, :, rank:])
        return dot3(top, own) + dot3(bottom, partner)

    def consume(unit):
        level, group = units[unit]
        own_copy(unit).wait()

        def landed(index, carry):
            arrive(unit, index * CORES + 1 - core)
            return carry

        lax.fori_loop(0, chips, landed, 0)
        if level == 0:
            load(group).wait()
        tiles = cols // tile
        if level < local_levels:
            stride = 1 << level

            def pair(index, carry):
                low = index // stride * 2 * stride + index % stride
                high = low + stride

                def part(step, inner):
                    at = pl.ds(pl.multiple_of(step * tile, tile), tile)
                    first = split(state[low, group, :, at])
                    second = split(state[high, group, :, at])
                    state[low, group, :, at] = product(level, group, low, first, second)
                    state[high, group, :, at] = product(level, group, high, second, first)
                    return inner

                lax.fori_loop(0, tiles, part, 0)
                pass_on(level, group, low)
                pass_on(level, group, high)
                return carry

            lax.fori_loop(0, nloc // 2, pair, 0)
        else:
            half = max(nloc // 2, 1)

            def single(step, carry):
                block = step % 2 * half + step // 2
                exchange(level, group, block).wait()

                def part(step, inner):
                    at = pl.ds(pl.multiple_of(step * tile, tile), tile)
                    first = split(state[block, group, :, at])
                    second = split(other[level - local_levels, block, group, :, at])
                    state[block, group, :, at] = product(level, group, block, first, second)
                    return inner

                lax.fori_loop(0, tiles, part, 0)
                pass_on(level, group, block)
                return carry

            lax.fori_loop(0, nloc, single, 0)

    for group in range(groups):
        load(group).start()
    for unit in range(min(AHEAD, len(units))):
        send_own(unit)
    if local_levels == 0:
        for group in range(groups):
            load(group).wait()
            for block in range(nloc):
                exchange(0, group, block).start()
    due = sorted((unit + LAG[units[unit][0]], unit) for unit in range(len(units)))
    for unit in range(len(units)):
        relay(unit)
        if unit + AHEAD < len(units):
            send_own(unit + AHEAD)
        while due and due[0][0] <= unit:
            consume(due.pop(0)[1])
    while due:
        consume(due.pop(0)[1])

    for group in range(groups):
        for block in range(nloc):
            store(group, block).wait()
    for unit in range(len(units)):

        def drained(index, carry):
            source = index * CORES + core
            done = functools.partial(remote, unit, shard(unit, source), source)

            @pl.when((index <= chip) & (chip < chips - 1))
            def _():
                done(UP, sibling).wait_send()

            @pl.when((index >= chip) & (chip > 0))
            def _():
                done(DOWN, sibling).wait_send()

            done(SIDE, sibling).wait_send()
            return carry

        lax.fori_loop(0, chips, drained, 0)


def body(coeff, factors):
    blocks, rank, cols = coeff.shape
    rows, width = factors.shape[2:]
    groups = 1 << (BITS - LEVELS)
    nloc = blocks // groups
    local_levels = nloc.bit_length() - 1
    devices = lax.axis_size("exc")
    units = LEVELS * groups
    crossing = LEVELS - local_levels
    dma = pltpu.SemaphoreType.DMA
    result = pl.pallas_call(
        functools.partial(kernel, local_levels),
        out_shape=jax.ShapeDtypeStruct((nloc, groups, rank, cols), jnp.float32),
        in_specs=[pl.BlockSpec(memory_space=pl.ANY)] * 2,
        out_specs=pl.BlockSpec(memory_space=pl.ANY),
        scratch_shapes=[
            pltpu.VMEM((LEVELS, nloc, groups, rank, width), jnp.float32),
            pltpu.VMEM((crossing, nloc, groups, rank, cols), jnp.float32),
            pltpu.VMEM((nloc, groups, rank, cols), jnp.float32),
            dma((groups,)),
            dma((groups, nloc)),
            dma((units,)),
            dma((units, devices)),
            dma((units, 3, devices // CORES)),
            dma((crossing, groups, nloc)),
            dma((crossing, groups, nloc)),
        ],
        compiler_params=pltpu.CompilerParams(has_side_effects=True, vmem_limit_bytes=63 << 20),
    )(
        coeff.reshape(nloc, groups, rank, cols),
        factors.reshape(LEVELS, nloc, groups, rows, width),
    )
    return result.reshape(coeff.shape)


def solution(mesh):
    return jax.shard_map(
        body,
        mesh=mesh,
        in_specs=(P("space", None, "exc"), P(None, "space", "exc", None)),
        out_specs=P("space", None, "exc"),
        check_vma=False,
    )
```
